256 devices in a mesh: band: 64 (over z_lo, x, y, core), sector: 4 (over z_hi).
Axes of the slice: x: 4, y: 4, z: 8 (z_hi: 4, z_lo: 2; z = z_hi * 2 + z_lo), core: 2. Of those that a mesh axis runs over, the one named last changes fastest.
Arguments:
- field: bfloat16 [64, 1440, 72], P('band', 'sector'), may hold values from -6 to 6
- filters: float32 [9, 64, 3, 17], P(None, 'band'), may hold values from -1.2 to 1.2
- reach: int32 [64], P('band'), may hold values from 1 to 8, as said below
- w_enc: bfloat16 [9, 72, 384], replicated, may hold values from -0.25 to 0.25
- gain: float32 [384], replicated, may hold values from 0.5 to 1.5
- w_qkv: bfloat16 [384, 1152], replicated, may hold values from -0.3125 to 0.3125
- w_out: bfloat16 [384, 384], replicated, may hold values from -0.3125 to 0.3125
- tau: float32 [8], replicated, may hold values from 0.25 to 24
- neighbours: int32 [64, 4, 3, 4], P('band', 'sector'), may hold values from 0 to 1, as said below
Outputs:
- output: bfloat16 [64, 1440, 384], P('band', 'sector')
The draws below stay inside these ranges and needn't reach their ends.
Inputs may be any that keep to these rules, and one draw needn't show every extreme that they name: reach[i] is the filter's longitude reach in row i; it equals 8 in the first and last row. neighbours[b, s, r, t] is 1 where query block (b, s) attends key row b - 1 + r in sector t; it is 1 for the block's own rows in its own sector and 0 for rows outside the grid.
All inputs are finite; a program needn't handle non-finite values.
Results may differ from the reference program's by a relative error of at most 0.03.
Values may be sent and summed in bfloat16 or wider, within the bound.
No kernel may reach another device: no remote copies, remote signals or barrier semaphores. Data moves between devices by JAX's collectives and lax.ppermute only.
A program may use at most 64 MiB of HBM per device.

```python
import math
import jax
import jax.numpy as jnp
from jax import lax

ROWS_DEV = 1
LON_DEV = 360
C_IN = 72
D = 384
HEADS = 8
K = 9
FR = 1
LW = 8
KH = 1
KROWS = 3
NLAT = 64
NLON = 1440
N_BAND = 64
N_SECTOR = 4


def draw_reach(key, part):
    values = jax.random.randint(key, (NLAT,), 1, LW + 1).astype(jnp.int32)
    values = values.at[0].set(LW)
    return values.at[NLAT - 1].set(LW)


def draw_neighbours(key, part):
    band_ids = jnp.arange(N_BAND, dtype=jnp.int32).reshape(N_BAND, 1, 1, 1)
    sector_ids = jnp.arange(N_SECTOR, dtype=jnp.int32).reshape(1, N_SECTOR, 1, 1)
    offsets = jnp.arange(KROWS, dtype=jnp.int32).reshape(1, 1, KROWS, 1)
    targets = jnp.arange(N_SECTOR, dtype=jnp.int32).reshape(1, 1, 1, N_SECTOR)
    row_ids = band_ids * ROWS_DEV - KH + offsets
    inside = (row_ids >= 0) & (row_ids < NLAT)
    own_rows = (offsets >= KH) & (offsets < KH + ROWS_DEV)
    distance = jnp.minimum((targets - sector_ids) % N_SECTOR, (sector_ids - targets) % N_SECTOR)
    edge = max(1, N_BAND // 8)
    polar = (band_ids < edge) | (band_ids >= N_BAND - edge)
    coins = jax.random.randint(key, (N_BAND, N_SECTOR, KROWS, N_SECTOR), 0, 2)
    keep = polar | (distance <= 1) & (coins == 1) | (distance == 0) & own_rows
    return (inside & keep).astype(jnp.int32)


def level_of(key, extent, pieces, smallest, top_value):
    loudness, own = 1.0, jax.random.fold_in(key, 6)
    for axis_at, shards_of in pieces:
        steps = jnp.exp(jax.random.uniform(jax.random.fold_in(own, axis_at), (shards_of,), jnp.float32, smallest / len(pieces), top_value / len(pieces)))
        loudness = loudness * jnp.repeat(steps, extent[axis_at] // shards_of).reshape([-1 if axis == axis_at else 1 for axis in range(len(extent))])
    return loudness


def scatter_about(own_key, extent, scale, bound, cuts=(), held_as=jnp.bfloat16):
    drawn = scale * jax.random.normal(own_key, extent, jnp.float32)
    if cuts:
        drawn = drawn * level_of(own_key, extent, cuts, -0.22, 0.18)
    return jnp.clip(drawn, -bound, bound).astype(held_as)


def setup_inputs(seed: int = 0) -> dict:
    key_list = jax.random.split(jax.random.key(seed), 10)
    return {
        "field": scatter_about(key_list[0], (NLAT, NLON, C_IN), 1.0, 6.0, ((0, 64), (1, 4))),
        "filters": scatter_about(key_list[1], (K, NLAT, 2 * FR + 1, 2 * LW + 1), 0.2, 1.2, ((1, 64),), jnp.float32),
        "reach": draw_reach(jax.random.fold_in(key_list[9], 71), 0),
        "w_enc": scatter_about(key_list[3], (K, C_IN, D), (K * C_IN) ** -0.5, 0.25),
        "gain": jnp.clip(1.0 + 0.1 * jax.random.normal(key_list[4], (D,), jnp.float32), 0.5, 1.5),
        "w_qkv": scatter_about(key_list[5], (D, 3 * D), D ** -0.5, 0.3125),
        "w_out": scatter_about(key_list[6], (D, D), D ** -0.5, 0.3125),
        "tau": jnp.clip(jnp.exp(jax.random.uniform(key_list[7], (HEADS,), jnp.float32, math.log(0.25), math.log(24.0))), 0.25, 24.0),
        "neighbours": draw_neighbours(jax.random.fold_in(key_list[9], 71), 0),
    }


def rotate(values, row_ids, col_ids, nlat, nlon):
    npair = values.shape[-1] // 2
    nhalf = npair // 2
    index = jnp.arange(npair, dtype=jnp.int32)
    lon_freq = jnp.where(index < nhalf, index + 1, 0).astype(jnp.float32)
    lat_freq = jnp.where(index >= nhalf, index - nhalf + 1, 0).astype(jnp.float32)
    lon_angle = 2.0 * math.pi / nlon * col_ids.astype(jnp.float32)
    lat_angle = math.pi / nlat * (row_ids.astype(jnp.float32) + 0.5)
    angle = lat_angle[:, None, None] * lat_freq + lon_angle[None, :, None] * lon_freq
    cosine = jnp.cos(angle)[:, :, None, :]
    sine = jnp.sin(angle)[:, :, None, :]
    first = values[..., :npair]
    second = values[..., npair:]
    return jnp.concatenate([first * cosine - second * sine, first * sine + second * cosine], -1)

def normalize(hidden, gain):
    values = hidden.astype(jnp.float32)
    meansquare = lax.optimization_barrier(jnp.mean(values * values, -1, keepdims=True))
    return (values * lax.rsqrt(meansquare + 1e-05) * gain).astype(jnp.bfloat16)

def reference(field, filters, reach, w_enc, gain, w_qkv, w_out, tau, neighbours):
    head_dim = D // HEADS
    padded = jnp.pad(field, ((FR, FR), (0, 0), (0, 0)))
    wrapped = jnp.concatenate([padded[:, NLON - LW:], padded, padded[:, :LW]], 1)
    offsets = jnp.abs(jnp.arange(2 * LW + 1, dtype=jnp.int32) - LW)
    tap_keep = (offsets[None, :] <= reach[:, None]).astype(jnp.float32)
    tap_weights = filters * tap_keep[None, :, None, :]
    columns = jnp.arange(NLON, dtype=jnp.int32)

    def encode_row(row_id):
        window = lax.dynamic_slice_in_dim(wrapped, row_id, 2 * FR + 1, 0)
        shifted = jnp.stack([window[:, shift:shift + NLON] for shift in range(2 * LW + 1)], 1)
        weights_row = lax.dynamic_index_in_dim(tap_weights, row_id, 1, keepdims=False)
        conv = jnp.einsum('kab,abjc->kjc', weights_row, shifted.astype(jnp.float32), precision=lax.Precision.HIGHEST).astype(jnp.bfloat16)
        hidden = jax.nn.gelu(jnp.einsum('kjc,kcd->jd', conv.astype(jnp.float32), w_enc.astype(jnp.float32))).astype(jnp.bfloat16)
        normed = normalize(hidden, gain)
        proj = jnp.dot(normed, w_qkv, preferred_element_type=jnp.float32).reshape(1, NLON, 3, HEADS, head_dim)
        row_ids = jnp.reshape(row_id, (1,))
        query = rotate(proj[:, :, 0], row_ids, columns, NLAT, NLON).astype(jnp.bfloat16)[0]
        key = rotate(proj[:, :, 1], row_ids, columns, NLAT, NLON).astype(jnp.bfloat16)[0]
        value = proj[0, :, 2].astype(jnp.bfloat16)
        return (hidden, query, key, value)
    hidden, query, key, value = lax.map(encode_row, jnp.arange(NLAT, dtype=jnp.int32))
    key_pad = jnp.pad(key, ((KH, KH), (0, 0), (0, 0), (0, 0)))
    value_pad = jnp.pad(value, ((KH, KH), (0, 0), (0, 0), (0, 0)))
    scale = tau.astype(jnp.float32)[:, None, None] / math.sqrt(head_dim)

    def attend_tile(tile):
        band_id = tile // N_SECTOR
        sector_id = tile % N_SECTOR
        start_row = (band_id * ROWS_DEV).astype(jnp.int32)
        start_col = (sector_id * LON_DEV).astype(jnp.int32)
        zero = jnp.zeros((), jnp.int32)
        q_tile = lax.dynamic_slice(query, (start_row, start_col, zero, zero), (ROWS_DEV, LON_DEV, HEADS, head_dim))
        k_tile = lax.dynamic_slice(key_pad, (start_row, zero, zero, zero), (KROWS, NLON, HEADS, head_dim))
        v_tile = lax.dynamic_slice(value_pad, (start_row, zero, zero, zero), (KROWS, NLON, HEADS, head_dim))
        h_tile = lax.dynamic_slice(hidden, (start_row, start_col, zero), (ROWS_DEV, LON_DEV, D))
        allowed = neighbours[band_id, sector_id]
        keymask = jnp.repeat(allowed, LON_DEV, axis=1).reshape(-1) > 0
        q_flat = q_tile.reshape(ROWS_DEV * LON_DEV, HEADS, head_dim).astype(jnp.float32)
        k_flat = k_tile.reshape(KROWS * NLON, HEADS, head_dim).astype(jnp.float32)
        v_flat = v_tile.reshape(KROWS * NLON, HEADS, head_dim).astype(jnp.float32)
        scores = jnp.einsum('qhd,khd->hqk', q_flat, k_flat) * scale
        scores = jnp.where(keymask[None, None, :], scores, -1e+30)
        peak = lax.optimization_barrier(jnp.max(scores, -1, keepdims=True))
        expo = jnp.exp(scores - peak)
        total = lax.optimization_barrier(jnp.sum(expo, -1, keepdims=True))
        weights = expo.astype(jnp.bfloat16).astype(jnp.float32)
        attended = jnp.einsum('hqk,khd->hqd', weights, v_flat) / total
        attended = jnp.transpose(attended, (1, 0, 2)).reshape(ROWS_DEV * LON_DEV, D).astype(jnp.bfloat16)
        mixed = jnp.dot(attended, w_out, preferred_element_type=jnp.float32)
        return (h_tile.astype(jnp.float32) + mixed.reshape(ROWS_DEV, LON_DEV, D)).astype(jnp.bfloat16)
    tiles = lax.map(attend_tile, jnp.arange(N_BAND * N_SECTOR, dtype=jnp.int32))
    tiles = tiles.reshape(N_BAND, N_SECTOR, ROWS_DEV, LON_DEV, D)
    return jnp.transpose(tiles, (0, 2, 1, 3, 4)).reshape(NLAT, NLON, D)
```

```python
import functools
import math

import jax
import jax.numpy as jnp
import numpy as np
from jax import lax
from jax.experimental import pallas as pl
from jax.experimental.pallas import tpu as pltpu
from jax.sharding import PartitionSpec as P

BF = jnp.bfloat16
F32 = jnp.float32
HEADS, HD, D, CIN, NK = 8, 48, 384, 72, 9
LON, LANES, NSEC, NROW = 360, 384, 4, 3
WIDE = NSEC * LANES
CP = 80
NEG = -1e30


def rope_tables():
    pair = np.arange(24)
    lane = np.arange(WIDE)
    lon = (lane // LANES) * LON + lane % LANES
    angle = 2.0 * math.pi / 1440 * lon[None, :] * np.where(pair < 12, pair + 1, 0)[:, None]
    lon_tab = np.stack([np.cos(angle), np.sin(angle)]).astype(np.float32)
    offs = np.arange(NROW) - 1
    lat = math.pi / 64 * offs[:, None] * np.where(pair >= 12, pair - 11, 0)[None, :]
    lat_tab = np.stack([np.cos(lat), np.sin(lat)], 1).astype(np.float32)
    lat_tab = np.broadcast_to(lat_tab[..., None], (NROW, 2, 24, 128))
    return lon_tab, np.ascontiguousarray(lat_tab)


def dot(a, b):
    return jnp.dot(a, b, preferred_element_type=F32)


def window_kernel(keep, rm2, rm1, r0, rp1, rp2, wenc, wqkv, wout, lon_tab, lat_tab, out,
                  ff, taps, toep, gath, conv, norm, keys, vals, qs, hid_own, att):
    raw = (rm2, rm1, r0, rp1, rp2)
    lane = lax.broadcasted_iota(jnp.int32, (CP, 128), 1)
    for row in range(5):
        for u in range(NSEC):
            left = raw[row][(u + 3) % 4, :, 256:384].astype(F32)
            right = raw[row][(u + 1) % 4, :, 0:128].astype(F32)
            first = raw[row][u, :, 0:128].astype(F32)
            last = raw[row][u, :, 256:384].astype(F32)
            first = jnp.where(lane < 8, pltpu.roll(left, 24, 1), first)
            turned = pltpu.roll(right, 104, 1)
            last = jnp.where((lane >= 112) & (lane < 120), turned, last)
            ff[row, u, :, 0:128] = first.astype(BF)
            ff[row, u, :, 128:256] = raw[row][u, :, 128:256]
            ff[row, u, :, 256:384] = last.astype(BF)
    for row in range(NROW):
        for k in range(NK):
            block = raw[row + 1][k // 8, 72:80, :].astype(F32)
            for a in range(3):
                taps[row, k * 3 + a : k * 3 + a + 1, :] = block[
                    k % 8 : k % 8 + 1, a * 128 : a * 128 + 128
                ]
    toep[432:512, :] = jnp.zeros((80, NK * 128), BF)
    jp = lax.broadcasted_iota(jnp.int32, (128, 128), 0)
    jj = lax.broadcasted_iota(jnp.int32, (128, 128), 1)
    lon_pair = lax.broadcasted_iota(jnp.int32, (24, 128), 0) < 12
    sub16 = lax.broadcasted_iota(jnp.int32, (16, LANES), 0)
    lane16 = lax.broadcasted_iota(jnp.int32, (16, LANES), 1)

    def rotate(x, c, s):
        x1, x2 = x[0:24], x[24:48]
        return jnp.concatenate([x1 * c - x2 * s, x1 * s + x2 * c], 0)

    def encode(r, carry):
        tp = taps[r]
        for k in range(NK):
            for a in range(3):
                i = k * 3 + a
                base = jnp.broadcast_to(tp[i : i + 1, :], (128, 128))
                circ = pltpu.roll(base, 0, 1, stride=1, stride_axis=0)
                main = jnp.where(jj <= jp, circ, 0.0).astype(BF)
                tail = jnp.where(jj > jp, circ, 0.0)[0:16].astype(BF)
                toep[a * 128 : a * 128 + 128, k * 128 : k * 128 + 128] = main
                toep[384 + a * 16 : 400 + a * 16, k * 128 : k * 128 + 128] = tail
        for u in range(NSEC):
            for t in range(3):
                at = (u * 3 + t) * CP
                for a in range(3):
                    gath[at : at + CP, a * 128 : a * 128 + 128] = ff[
                        r + a, u, :, t * 128 : t * 128 + 128
                    ]
                if t < 2:
                    nxt = [
                        ff[r + a, u, :, t * 128 + 128 : t * 128 + 256].astype(F32) for a in range(3)
                    ]
                    rest = jnp.where(
                        lane < 32, pltpu.roll(nxt[1], 16, 1), pltpu.roll(nxt[2], 32, 1)
                    )
                    rest = jnp.where(lane < 16, nxt[0], rest)
                    gath[at : at + CP, 384:512] = rest.astype(BF)
                else:
                    gath[at : at + CP, 384:512] = jnp.zeros((CP, 128), BF)
        for kk in range(5):
            lo, hi = kk * 256, min(kk * 256 + 256, NK * 128)
            got = dot(gath[...], toep[:, lo:hi]).astype(BF)
            for k in range(2 * kk, min(2 * kk + 2, NK)):
                sub = got[:, (k - 2 * kk) * 128 : (k - 2 * kk) * 128 + 128]
                for t in range(12):
                    conv[k * CP : k * CP + CP, t * 128 : t * 128 + 128] = sub[t * CP : t * CP + CP]

        for n in range(3):
            cols = slice(n * 512, n * 512 + 512)
            pre = dot(wenc[...], conv[:, cols])
            inner = pre * (0.7978845608028654 + 0.035677408136300125 * (pre * pre))
            half = 0.5 * pre
            hid = half + half * jnp.tanh(inner)
            hid = hid.astype(BF).astype(F32)
            scale = lax.rsqrt(jnp.sum(hid * hid, 0, keepdims=True) * (1.0 / D) + 1e-5)
            norm[:, cols] = (hid * scale).astype(BF)
            if n == 0:
                @pl.when(r == 1)
                def _():
                    hid_own[...] = hid[:, 0:LANES]
        lat_c, lat_s = lat_tab[r, 0], lat_tab[r, 1]

        for n in range(3):
            cols = slice(n * 512, n * 512 + 512)
            kv = dot(wqkv[D : 3 * D, :], norm[:, cols])
            cos = jnp.concatenate(
                [jnp.where(lon_pair, lon_tab[0, :, n * 512 + i * 128 : n * 512 + i * 128 + 128], lat_c) for i in range(4)], 1)
            sin = jnp.concatenate(
                [jnp.where(lon_pair, lon_tab[1, :, n * 512 + i * 128 : n * 512 + i * 128 + 128], lat_s) for i in range(4)], 1)
            for h in range(HEADS):
                kh = rotate(kv[h * HD : h * HD + HD], cos, sin)
                keys[r, h, 0:HD, cols] = kh.astype(BF)
                vals[r, h, 0:HD, cols] = kv[D + h * HD : D + h * HD + HD].astype(BF)
        ones = jnp.where(sub16 == 0, 1.0, 0.0).astype(BF)
        for u in range(NSEC):
            ok = jnp.where(keep[r * NSEC + u] > 0, LON, 0)
            bias = jnp.where((sub16 == 0) & (lane16 >= ok), NEG, 0.0).astype(BF)
            for h in range(HEADS):
                keys[r, h, HD:64, u * LANES : u * LANES + LANES] = bias
                vals[r, h, HD:64, u * LANES : u * LANES + LANES] = ones

        @pl.when(r == 1)
        def _():
            qt = dot(wqkv[0:D, :], norm[:, 0:LANES])
            cos = jnp.concatenate(
                [jnp.where(lon_pair, lon_tab[0, :, i * 128 : i * 128 + 128], lat_c) for i in range(3)], 1)
            sin = jnp.concatenate(
                [jnp.where(lon_pair, lon_tab[1, :, i * 128 : i * 128 + 128], lat_s) for i in range(3)], 1)
            unit = jnp.where(sub16 == 0, 1.0, 0.0)
            for h in range(HEADS):
                qh = rotate(qt[h * HD : h * HD + HD], cos, sin)
                qh = jnp.concatenate([qh, unit], 0)
                qs[h] = jnp.transpose(qh)[0:LON].astype(BF)

        return carry

    lax.fori_loop(0, NROW, encode, 0)

    QB = 120

    def attend(h2, carry):
        for b in range(LON // QB):
            pieces = []
            for hh in range(2):
                h = h2 * 2 + hh
                q = qs[h, b * QB : b * QB + QB, :]
                s = [dot(q, keys[r, h]) for r in range(NROW)]
                peak = jnp.max(jnp.maximum(jnp.maximum(s[0], s[1]), s[2]), 1, keepdims=True)
                acc = jnp.zeros((QB, 64), F32)
                for r in range(NROW):
                    w = jnp.exp2(s[r] - peak).astype(BF)
                    acc = acc + lax.dot_general(
                        w, vals[r, h], (((1,), (1,)), ((), ())), preferred_element_type=F32
                    )
                pieces.append(acc / acc[:, HD : HD + 1])
            att[h2, b * QB : b * QB + QB, :] = jnp.concatenate(pieces, 1).astype(BF)
        return carry

    lax.fori_loop(0, HEADS // 2, attend, 0)
    mixed = dot(att[0], wout[0:128, :])
    for i in range(1, 4):
        mixed = mixed + dot(att[i], wout[i * 128 : i * 128 + 128, :])
    hid_nat = jnp.transpose(hid_own[...])[0:LON]
    out[...] = (hid_nat + mixed).astype(BF)


def window_call(keep, rows, wenc, wqkv, wout):
    lon_tab, lat_tab = rope_tables()
    vm = pl.BlockSpec(memory_space=pltpu.VMEM)
    return pl.pallas_call(
        window_kernel,
        out_shape=jax.ShapeDtypeStruct((LON, D), BF),
        in_specs=[pl.BlockSpec(memory_space=pltpu.SMEM)] + [vm] * 10,
        out_specs=vm,
        scratch_shapes=[
            pltpu.VMEM((5, NSEC, CP, LANES), BF),
            pltpu.VMEM((NROW, 32, 128), F32),
            pltpu.VMEM((512, NK * 128), BF),
            pltpu.VMEM((12 * CP, 512), BF),
            pltpu.VMEM((NK * CP, WIDE), BF),
            pltpu.VMEM((D, WIDE), BF),
            pltpu.VMEM((NROW, HEADS, 64, WIDE), BF),
            pltpu.VMEM((NROW, HEADS, 64, WIDE), BF),
            pltpu.VMEM((HEADS, LON, 64), BF),
            pltpu.VMEM((D, LANES), F32),
            pltpu.VMEM((4, LON, 128), BF),
        ],
        compiler_params=pltpu.CompilerParams(vmem_limit_bytes=60 * 1024 * 1024),
        name="window",
    )(keep, *rows, wenc, wqkv, wout, jnp.asarray(lon_tab), jnp.asarray(lat_tab))


def prepare_weights(w_enc, gain, w_qkv, w_out, tau):
    wenc = jnp.pad(jnp.transpose(w_enc, (2, 0, 1)), ((0, 0), (0, 0), (0, CP - CIN))).reshape(D, NK * CP)
    scale = jnp.repeat(tau * (math.log2(math.e) / math.sqrt(HD)), HD)
    cols = jnp.concatenate([scale, jnp.ones((2 * D,), F32)])
    wqkv = (w_qkv.astype(F32) * gain[:, None] * cols[None, :]).astype(BF).T
    wout = jnp.pad(w_out.reshape(HEADS, HD, D), ((0, 0), (0, 64 - HD), (0, 0))).reshape(512, D)
    return wenc, wqkv, wout


def prepare_taps(filters, reach):
    f = filters[:, 0]
    offsets = jnp.abs(jnp.arange(17, dtype=jnp.int32) - 8)
    f = jnp.where(offsets[None, None, :] <= reach[0], f, 0.0)
    base = jnp.concatenate(
        [f[:, :, 0:1], jnp.zeros((NK, 3, 111), F32), f[:, :, :0:-1]], -1
    ).reshape(NK, LANES)
    base = jnp.pad(base, ((0, 32 - NK), (0, 0))).astype(BF)
    return base.reshape(4, 8, LANES)


def prepare_field(field):
    return jnp.pad(field[0].T, ((0, 0), (8, LANES - LON - 8)))


def rel_keep(neighbours, s):
    nb = neighbours[0, 0]
    two = jnp.concatenate([nb, nb], 1)
    return lax.dynamic_slice(two, (0, s), (NROW, NSEC)).reshape(NROW * NSEC)


def local(field, filters, reach, w_enc, gain, w_qkv, w_out, tau, neighbours):
    nb, ns = lax.axis_size("band"), lax.axis_size("sector")
    own = prepare_field(field)
    got = [lax.ppermute(own, "sector", [((i + u) % ns, i) for i in range(ns)]) for u in (1, 2, 3)]
    row = jnp.concatenate([jnp.stack([own] + got), prepare_taps(filters, reach)], 1)

    def shifted(d):
        return lax.ppermute(row, "band", [(i + d, i) for i in range(nb) if 0 <= i + d < nb])

    rows = [shifted(-2), shifted(-1), row, shifted(1), shifted(2)]
    keep = rel_keep(neighbours, lax.axis_index("sector"))
    return window_call(keep, rows, *prepare_weights(w_enc, gain, w_qkv, w_out, tau))[None]


def solution(mesh):
    return jax.shard_map(
        local,
        mesh=mesh,
        in_specs=(
            P("band", "sector", None),
            P(None, "band", None, None),
            P("band"),
            P(),
            P(),
            P(),
            P(),
            P(),
            P("band", "sector", None, None),
        ),
        out_specs=P("band", "sector", None),
        check_vma=False,
    )
```

```python
import math

import jax
import jax.numpy as jnp
import numpy as np
from jax import lax
from jax.experimental import pallas as pl
from jax.experimental.pallas import tpu as pltpu
from jax.sharding import PartitionSpec as P

BF = jnp.bfloat16
F32 = jnp.float32
HEADS, HD, D, CIN, NK = 8, 48, 384, 72, 9
LON, LANES, NSEC, NROW = 360, 384, 4, 3
NLON, NLAT = 1440, 64
WIDE = NSEC * LANES
CP = 80
HR = 64
NEG = -1e30


def lon_table():
    pair = np.arange(24)
    lane = np.arange(7 * LANES)
    lon = ((lane // LANES) % NSEC) * LON + lane % LANES
    angle = 2.0 * math.pi / NLON * lon[None, :] * np.where(pair < 12, pair + 1, 0)[:, None]
    return np.stack([np.cos(angle), np.sin(angle)]).astype(np.float32)


def lat_table():
    pair = np.arange(24)
    row = np.arange(NLAT + 2) - 1
    lat = math.pi / NLAT * (row[:, None] + 0.5) * np.where(pair >= 12, pair - 11, 0)[None, :]
    return np.stack([np.cos(lat), np.sin(lat)], 1).astype(np.float32)


def dot(a, b):
    return jnp.dot(a, b, preferred_element_type=F32)


def make_encoder(own):
    def kernel(odd, fa, fb, fc, wenc, wqkv, gain, tab, kv_out, *rest):
        if own:
            q_out, hid_out, ff, toep, gath, conv, norm = rest
        else:
            ff, toep, gath, conv, norm = rest
        raw = (fa, fb, fc)
        lane = lax.broadcasted_iota(jnp.int32, (CP, 128), 1)
        for row in range(3):
            for u in range(NSEC):
                left = raw[row][(u + 3) % 4, :, 256:384].astype(F32)
                right = raw[row][(u + 1) % 4, :, 0:128].astype(F32)
                first = raw[row][u, :, 0:128].astype(F32)
                last = raw[row][u, :, 256:384].astype(F32)
                first = jnp.where(lane < 8, pltpu.roll(left, 24, 1), first)
                turned = pltpu.roll(right, 104, 1)
                last = jnp.where((lane >= 112) & (lane < 120), turned, last)
                ff[row, u, :, 0:128] = first.astype(BF)
                ff[row, u, :, 128:256] = raw[row][u, :, 128:256]
                ff[row, u, :, 256:384] = last.astype(BF)
        toep[432:512, :] = jnp.zeros((80, NK * 128), BF)
        jp = lax.broadcasted_iota(jnp.int32, (128, 128), 0)
        jj = lax.broadcasted_iota(jnp.int32, (128, 128), 1)
        flip = odd[0] > 0
        for k in range(NK):
            block = fb[k // 8, 72:80, :].astype(F32)[k % 8 : k % 8 + 1]
            for a in range(3):
                tap = jnp.where(
                    flip,
                    block[:, (2 - a) * 128 : (2 - a) * 128 + 128],
                    block[:, a * 128 : a * 128 + 128],
                )
                circ = pltpu.roll(
                    jnp.broadcast_to(tap, (128, 128)), 0, 1, stride=1, stride_axis=0
                )
                main = jnp.where(jj <= jp, circ, 0.0).astype(BF)
                tail = jnp.where(jj > jp, circ, 0.0)[0:16].astype(BF)
                toep[a * 128 : a * 128 + 128, k * 128 : k * 128 + 128] = main
                toep[384 + a * 16 : 400 + a * 16, k * 128 : k * 128 + 128] = tail
        for u in range(NSEC):
            for t in range(3):
                at = (u * 3 + t) * CP
                for a in range(3):
                    gath[at : at + CP, a * 128 : a * 128 + 128] = ff[
                        a, u, :, t * 128 : t * 128 + 128
                    ]
                if t < 2:
                    nxt = [ff[a, u, :, t * 128 + 128 : t * 128 + 256].astype(F32) for a in range(3)]
                    rest_ = jnp.where(
                        lane < 32, pltpu.roll(nxt[1], 16, 1), pltpu.roll(nxt[2], 32, 1)
                    )
                    rest_ = jnp.where(lane < 16, nxt[0], rest_)
                    gath[at : at + CP, 384:512] = rest_.astype(BF)
                else:
                    gath[at : at + CP, 384:512] = jnp.zeros((CP, 128), BF)
        for kk in range(5):
            lo, hi = kk * 256, min(kk * 256 + 256, NK * 128)
            got = dot(gath[...], toep[:, lo:hi]).astype(BF)
            for k in range(2 * kk, min(2 * kk + 2, NK)):
                sub = got[:, (k - 2 * kk) * 128 : (k - 2 * kk) * 128 + 128]
                for t in range(12):
                    conv[k * CP : k * CP + CP, t * 128 : t * 128 + 128] = sub[t * CP : t * CP + CP]
        for n in range(3):
            cols = slice(n * 512, n * 512 + 512)
            pre = dot(wenc[...], conv[:, cols])
            inner = pre * (0.7978845608028654 + 0.035677408136300125 * (pre * pre))
            half = 0.5 * pre
            hid = half + half * jnp.tanh(inner)
            hid = hid.astype(BF).astype(F32)
            scale = lax.rsqrt(jnp.sum(hid * hid, 0, keepdims=True) * (1.0 / D) + 1e-5)
            for i in range(4):
                part = slice(i * 128, i * 128 + 128)
                norm[:, n * 512 + i * 128 : n * 512 + i * 128 + 128] = (
                    hid[:, part] * scale[:, part] * gain[...]
                ).astype(BF)
            if own and n == 0:
                hid_out[...] = jnp.transpose(hid[:, 0:LANES])[0:LON]

        def rotate(x, cols):
            c, s = tab[0, :, cols], tab[1, :, cols]
            x1, x2 = x[0:24], x[24:48]
            return jnp.concatenate([x1 * c - x2 * s, x1 * s + x2 * c], 0)

        sub16 = lax.broadcasted_iota(jnp.int32, (16, LANES), 0)
        lane16 = lax.broadcasted_iota(jnp.int32, (16, LANES), 1)
        if own:
            qt = dot(wqkv[0:D, :], norm[:, 0:LANES])
            zero = jnp.zeros((16, LANES), F32)
            for h in range(HEADS):
                qh = rotate(qt[h * HD : h * HD + HD], slice(0, LANES))
                q_out[h] = jnp.transpose(jnp.concatenate([qh, zero], 0))[0:LON].astype(BF)
        for n in range(3):
            cols = slice(n * 512, n * 512 + 512)
            kv = dot(wqkv[D : 3 * D, :], norm[:, cols])
            for h in range(HEADS):
                kv_out[0, h, 0:HD, cols] = rotate(kv[h * HD : h * HD + HD], cols).astype(BF)
                kv_out[1, h, 0:HD, cols] = kv[D + h * HD : D + h * HD + HD].astype(BF)
        ones = jnp.where(sub16 == 0, 1.0, 0.0).astype(BF)
        for u in range(NSEC):
            mark = (sub16 == u + 1) | ((sub16 == 0) & (lane16 >= LON))
            mark = jnp.where(mark, 1.0, 0.0).astype(BF)
            for h in range(HEADS):
                kv_out[0, h, HD:HR, u * LANES : u * LANES + LANES] = mark
                kv_out[1, h, HD:HR, u * LANES : u * LANES + LANES] = ones

    return kernel


def encode_call(own, odd, rows, wenc, wqkv, gain, tab):
    vm = pl.BlockSpec(memory_space=pltpu.VMEM)
    out_shape = [jax.ShapeDtypeStruct((2, HEADS, HR, WIDE), BF)]
    if own:
        out_shape += [
            jax.ShapeDtypeStruct((HEADS, LON, HR), BF),
            jax.ShapeDtypeStruct((LON, D), F32),
        ]
    return pl.pallas_call(
        make_encoder(own),
        out_shape=out_shape,
        in_specs=[pl.BlockSpec(memory_space=pltpu.SMEM)] + [vm] * 7,
        out_specs=[vm] * len(out_shape),
        scratch_shapes=[
            pltpu.VMEM((3, NSEC, CP, LANES), BF),
            pltpu.VMEM((512, NK * 128), BF),
            pltpu.VMEM((12 * CP, 512), BF),
            pltpu.VMEM((NK * CP, WIDE), BF),
            pltpu.VMEM((D, WIDE), BF),
        ],
        compiler_params=pltpu.CompilerParams(vmem_limit_bytes=24 * 1024 * 1024),
        cost_estimate=pl.CostEstimate(
            flops=5_000_000_000, bytes_accessed=6_000_000, transcendentals=600_000
        ),
        name="encode_own" if own else "encode_outer",
    )(odd, *rows, wenc, wqkv, gain, tab)


QB = 120


def attend_kernel(keep, temper, kv0, kv1, kv2, qs, hid, wout, out, att):
    kvs = (kv0, kv1, kv2)
    lane = lax.broadcasted_iota(jnp.int32, (1, HR), 1)
    bias = []
    for r in range(NROW):
        row = jnp.where(lane == HD, NEG, 0.0)
        for u in range(NSEC):
            off = jnp.where(keep[r * NSEC + u] > 0, 0.0, NEG)
            row = jnp.where(lane == HD + 1 + u, off, row)
        bias.append(row.astype(BF))

    def attend(h2, carry):
        for b in range(LON // QB):
            pieces = []
            for hh in range(2):
                h = h2 * 2 + hh
                q = qs[h, b * QB : b * QB + QB, :]
                s = [dot(q + bias[r], kvs[r][0, h]) for r in range(NROW)]
                peak = jnp.max(jnp.maximum(jnp.maximum(s[0], s[1]), s[2]), 1, keepdims=True)
                acc = jnp.zeros((QB, HR), F32)
                for r in range(NROW):
                    w = jnp.exp2((s[r] - peak) * temper[h]).astype(BF)
                    acc = acc + lax.dot_general(
                        w, kvs[r][1, h], (((1,), (1,)), ((), ())), preferred_element_type=F32
                    )
                pieces.append(acc / acc[:, HD : HD + 1])
            att[h2, b * QB : b * QB + QB, :] = jnp.concatenate(pieces, 1).astype(BF)
        return carry

    lax.fori_loop(0, HEADS // 2, attend, 0)
    mixed = dot(att[0], wout[0:128, :])
    for i in range(1, 4):
        mixed = mixed + dot(att[i], wout[i * 128 : i * 128 + 128, :])
    out[...] = (hid[...] + mixed).astype(BF)


def attend_call(keep, temper, kvs, qs, hid, wout):
    vm = pl.BlockSpec(memory_space=pltpu.VMEM)
    sm = pl.BlockSpec(memory_space=pltpu.SMEM)
    return pl.pallas_call(
        attend_kernel,
        out_shape=jax.ShapeDtypeStruct((LON, D), BF),
        in_specs=[sm, sm] + [vm] * 6,
        out_specs=vm,
        scratch_shapes=[pltpu.VMEM((4, LON, 128), BF)],
        compiler_params=pltpu.CompilerParams(vmem_limit_bytes=32 * 1024 * 1024),
        cost_estimate=pl.CostEstimate(
            flops=14_000_000_000, bytes_accessed=10_000_000, transcendentals=13_000_000
        ),
        name="attend",
    )(keep, temper, *kvs, qs, hid, wout)


def prepare_weights(w_enc, gain, w_qkv, w_out, tau):
    wenc = jnp.pad(jnp.transpose(w_enc, (2, 0, 1)), ((0, 0), (0, 0), (0, CP - CIN)))
    wenc = wenc.reshape(D, NK * CP)
    wout = jnp.pad(w_out.reshape(HEADS, HD, D), ((0, 0), (0, HR - HD), (0, 0)))
    wide_gain = jnp.broadcast_to(gain[:, None], (D, 128))
    temper = tau * (math.log2(math.e) / math.sqrt(HD))
    return wenc, w_qkv.T, wout.reshape(HEADS * HR, D), wide_gain, temper


def prepare_taps(filters, reach):
    f = filters[:, 0]
    offsets = jnp.abs(jnp.arange(17, dtype=jnp.int32) - 8)
    f = jnp.where(offsets[None, None, :] <= reach[0], f, 0.0)
    base = jnp.concatenate([f[:, :, 0:1], jnp.zeros((NK, 3, 111), F32), f[:, :, :0:-1]], -1)
    base = jnp.pad(base.reshape(NK, LANES), ((0, 32 - NK), (0, 0))).astype(BF)
    return base.reshape(4, 8, LANES)


def prepare_field(field):
    return jnp.pad(field[0].T, ((0, 0), (8, LANES - LON - 8)))


def rel_keep(neighbours, s, odd):
    nb = neighbours[0, 0]
    two = jnp.concatenate([nb, nb], 1)
    rel = lax.dynamic_slice(two, (0, s), (NROW, NSEC))
    outer = jnp.where(odd, rel[2], rel[0])
    inner = jnp.where(odd, rel[0], rel[2])
    return jnp.concatenate([rel[1], outer, inner])


def rotary(b, s, outer):
    lon = lax.dynamic_slice(jnp.asarray(lon_table()), (0, 0, s * LANES), (2, 24, WIDE))
    lat = jnp.asarray(lat_table())
    low = lax.broadcasted_iota(jnp.int32, (2, 24, WIDE), 1) < 12
    pick = lambda i: lax.dynamic_index_in_dim(lat, i + 1, 0, keepdims=False)[:, :, None]
    return [jnp.where(low, lon, pick(i)) for i in (b, outer)]


def local(field, filters, reach, w_enc, gain, w_qkv, w_out, tau, neighbours):
    nb, ns = lax.axis_size("band"), lax.axis_size("sector")
    b, s = lax.axis_index("band"), lax.axis_index("sector")
    odd = b % 2
    outer = b + 2 * odd - 1
    mine = prepare_field(field)
    got = [lax.ppermute(mine, "sector", [((i + u) % ns, i) for i in range(ns)]) for u in (1, 2, 3)]
    row = jnp.concatenate([jnp.stack([mine] + got), prepare_taps(filters, reach)], 1)
    side = [(i + 1 if i % 2 else i - 1, i) for i in range(nb)]
    side = [pair for pair in side if 0 <= pair[0] < nb]
    twin = [(i ^ 1, i) for i in range(nb)]
    near = lax.ppermute(row, "band", side)
    chip = lax.ppermute(row, "band", twin)
    far = lax.ppermute(chip, "band", side)
    wenc, wqkv, wout, wide_gain, temper = prepare_weights(w_enc, gain, w_qkv, w_out, tau)
    tabs = rotary(b, s, outer)
    flag = odd.astype(jnp.int32).reshape(1)
    kv_own, qs, hid = encode_call(True, flag, [near, row, chip], wenc, wqkv, wide_gain, tabs[0])
    kv_chip = lax.ppermute(kv_own, "band", twin)
    (kv_outer,) = encode_call(False, flag, [far, near, row], wenc, wqkv, wide_gain, tabs[1])
    keep = rel_keep(neighbours, s, odd == 1)
    return attend_call(keep, temper, [kv_own, kv_outer, kv_chip], qs, hid, wout)[None]


def solution(mesh):
    return jax.shard_map(
        local,
        mesh=mesh,
        in_specs=(
            P("band", "sector", None),
            P(None, "band", None, None),
            P("band"),
            P(),
            P(),
            P(),
            P(),
            P(),
            P("band", "sector", None, None),
        ),
        out_specs=P("band", "sector", None),
        check_vma=False,
    )
```
